512 devices in a mesh: tm: 8 (over z_lo), gx: 16 (over y, x), gy: 4 (over z_hi, core).
Axes of the slice: x: 4, y: 4, z: 16 (z_hi: 2, z_lo: 8; z = z_hi * 8 + z_lo), core: 2. Of those that a mesh axis runs over, the one named last changes fastest.
Arguments:
- start_states: float32 [8, 512, 64, 256], P('tm', 'gx', 'gy'), may hold values from 0.5 to 2
- wind_code: int32 [16, 4], P('gx', 'gy'), may hold values from 0 to 7
- wind_profile: float32 [2, 256], replicated, may hold values from 0.05 to 0.4
- vertical_mix: float32 [512, 64, 256], P('gx', 'gy'), may hold values from 0.01 to 0.1
Outputs:
- middle_states: float32 [8, 512, 64, 256], P('tm', 'gx', 'gy')
- final_states: float32 [8, 512, 64, 256], P('tm', 'gx', 'gy')
The draws below stay inside these ranges and needn't reach their ends.
Inputs may be any that keep to these rules, and one draw needn't show every extreme that they name: `wind_code`: a regime code.
All inputs are finite; a program needn't handle non-finite values.
Results may differ from the reference program's by a relative error of at most 0.00002.
Values sent between devices are 32-bit elements; how exact they have to be, the bound alone decides.
A program may use at most 64 MiB of HBM per device.

```python
import math
import jax
import jax.numpy as jnp
from jax import lax

BX = 32
BY = 16
NZ = 256
SWEEPS = 3
NX = 512
NY = 64
SLICES = 8


def touch_ends(drawn, own_key, least, high):
    longest = drawn.shape.index(max(drawn.shape))
    spots = []
    for shift in (0, 1):
        where = [jax.random.randint(jax.random.fold_in(own_key, axis), (), 0, length) for axis, length in enumerate(drawn.shape)]
        where[longest] = (where[longest] + shift) % drawn.shape[longest]
        spots.append(tuple(where))
    return drawn.at[spots[0]].set(least).at[spots[1]].set(high)


def steps_of(own_key, dims, split, low, high):
    factor_of, own = 1.0, jax.random.fold_in(own_key, 6)
    for axis_at, parts in split:
        steps = jnp.exp(jax.random.uniform(jax.random.fold_in(own, axis_at), (parts,), jnp.float32, low / len(split), high / len(split)))
        factor_of = factor_of * jnp.repeat(steps, dims[axis_at] // parts).reshape([-1 if axis == axis_at else 1 for axis in range(len(dims))])
    return factor_of


def setup_inputs(seed: int = 0) -> dict:
    splits = jax.random.split(jax.random.key(seed), 5)
    start_states = jnp.clip(0.5 + 1.5 * jax.random.uniform(splits[0], (SLICES, NX, NY, NZ), jnp.float32) ** steps_of(splits[0], (SLICES, NX, NY, NZ), ((0, 8), (1, 16), (2, 4)), -0.2, 0.2), 0.5, 2.0)
    wind_code = touch_ends(jax.random.randint(splits[1], (NX // BX, NY // BY), 0, 8), jax.random.fold_in(splits[1], 1), 0, 7).astype(jnp.int32)
    wind_profile = jnp.clip(jnp.exp(jax.random.uniform(splits[2], (2, NZ), jnp.float32, math.log(0.05), math.log(0.4))), 0.05, 0.4)
    vertical_mix = jnp.clip(jnp.exp(math.log(0.1) - 2.3025851 * jax.random.uniform(splits[3], (NX, NY, NZ), jnp.float32) ** steps_of(splits[3], (NX, NY, NZ), ((0, 16), (1, 4)), -0.2, 0.2)), 0.01, 0.1)
    return {"start_states": start_states, "wind_code": wind_code, "wind_profile": wind_profile, "vertical_mix": vertical_mix}


time_step = 0.5
half_step = 0.25
diffusion_low = 0.04
diffusion_high = 0.1
first_weights = (5.0 / 24.0, 1.0 / 3.0, -1.0 / 24.0)
second_weights = (-1.0 / 24.0, 1.0 / 3.0, 5.0 / 24.0)


def tendency(padded, sign_x, sign_y, strength, wind_profile, vertical_mix):
    row_count = padded.shape[0] - 4
    columns = padded.shape[1] - 4

    def neighbour(source, step_x, step_y):
        return source[2 + step_x:2 + step_x + row_count, 2 + step_y:2 + step_y + columns]

    centre = neighbour(padded, 0, 0)
    squared = padded * padded
    growth = squared / (1.0 + squared)
    growth_centre = neighbour(growth, 0, 0)
    spread = jnp.zeros_like(centre)
    for step_x, step_y in ((1, 0), (-1, 0), (0, 1), (0, -1)):
        weight = 0.5 + 0.5 * (growth_centre + neighbour(growth, step_x, step_y))
        spread = spread + weight * (neighbour(padded, step_x, step_y) - centre)
    upwind_x = jnp.where(sign_x > 0, neighbour(padded, -1, 0), neighbour(padded, 1, 0))
    farther_x = jnp.where(sign_x > 0, neighbour(padded, -2, 0), neighbour(padded, 2, 0))
    upwind_y = jnp.where(sign_y > 0, neighbour(padded, 0, -1), neighbour(padded, 0, 1))
    farther_y = jnp.where(sign_y > 0, neighbour(padded, 0, -2), neighbour(padded, 0, 2))
    carried = wind_profile[0] * (3.0 * centre - 4.0 * upwind_x + farther_x)
    carried = carried + wind_profile[1] * (3.0 * centre - 4.0 * upwind_y + farther_y)
    below_cells = jnp.concatenate([centre[:, :, :1], centre[:, :, :-1]], axis=2)
    above_cells = jnp.concatenate([centre[:, :, 1:], centre[:, :, -1:]], axis=2)
    return strength * spread - 0.5 * carried + vertical_mix * (below_cells + above_cells - 2.0 * centre)


def sweep_once(first_state, first_rate, slopes, tendency_of):
    middle = first_state + half_step * (first_rate - slopes[0]) + time_step * (
        first_weights[0] * slopes[0] + first_weights[1] * slopes[1] + first_weights[2] * slopes[2])
    middle_rate = tendency_of(middle)
    final_state = middle + half_step * (middle_rate - slopes[1]) + time_step * (
        second_weights[0] * slopes[0] + second_weights[1] * slopes[1] + second_weights[2] * slopes[2])
    final_rate = tendency_of(final_state)
    return (first_state, middle, final_state), (first_rate, middle_rate, final_rate)


def reference(start_states, wind_code, wind_profile, vertical_mix):
    regime = jnp.repeat(jnp.repeat(wind_code, BX, axis=0), BY, axis=1)[:, :, None]
    sign_x = 1.0 - 2.0 * (regime % 2).astype(jnp.float32)
    sign_y = 1.0 - 2.0 * ((regime // 2) % 2).astype(jnp.float32)
    strength = jnp.where(regime // 4 == 1, diffusion_high, diffusion_low)

    def tendency_of(state_field):
        padded = jnp.pad(state_field, ((2, 2), (2, 2), (0, 0)))
        return tendency(padded, sign_x, sign_y, strength, wind_profile, vertical_mix)

    def slice_step(previous, initial_state):
        initial_rate = tendency_of(initial_state)
        states = (initial_state, initial_state, initial_state)
        slopes = (initial_rate, initial_rate, initial_rate)
        finals = [initial_state]
        for sweep_index in range(SWEEPS):
            first_state = previous[sweep_index]
            first_rate = tendency_of(first_state)
            states, slopes = sweep_once(first_state, first_rate, slopes, tendency_of)
            finals.append(states[2])
        return jnp.stack(finals[:SWEEPS]), (states[1], states[2])

    carried_ends = jnp.broadcast_to(start_states[0], (SWEEPS,) + start_states.shape[1:])
    unused, outputs = lax.scan(slice_step, carried_ends, start_states)
    return outputs[0], outputs[1]
```

```python
import jax
import jax.numpy as jnp
from jax import lax
from jax.experimental import pallas as pl
from jax.experimental.pallas import tpu as pltpu
from jax.sharding import PartitionSpec as P

MESH = pl.DeviceIdType.MESH
time_step = 0.5
half_step = 0.25
diffusion_low = 0.04
diffusion_high = 0.1
first_weights = (5.0 / 24.0, 1.0 / 3.0, -1.0 / 24.0)
second_weights = (-1.0 / 24.0, 1.0 / 3.0, 5.0 / 24.0)
A = tuple(time_step * w - (half_step if i == 0 else 0.0) for i, w in enumerate(first_weights))
B = tuple(time_step * w - (half_step if i == 1 else 0.0) for i, w in enumerate(second_weights))

BX = 32
BY = 16
ROWS = 2 * BY
X0 = 2
R0 = 16
R1 = R0 + ROWS
FIELDS = 9
XUP, XDOWN, YUP, YDOWN, SHIFT, FORWARD = range(6)


def kernel(shape, start, code, profile, mixing, middle_out, final_out,
           u, h, vm, c1, c2, p1, p2, stage, out_stage, load_sem, store_sem, send_sem, recv_sem):
    nt, nx, ny = shape
    t, gx, gy = (lax.axis_index(a) for a in ("tm", "gx", "gy"))

    loads = []
    for k, source in enumerate((start.at[0], mixing)):
        for half in range(2):
            copy = pltpu.make_async_copy(
                source.at[:, :, pl.ds(128 * half, 128)], stage.at[k, half], load_sem.at[k, half])
            copy.start()
            loads.append(copy)

    def clear(x, carry):
        for l in range(FIELDS):
            u[l, x, pl.ds(R0 - 8, 8), :] = jnp.zeros((8, 128), jnp.float32)
            u[l, x, pl.ds(R1, 8), :] = jnp.zeros((8, 128), jnp.float32)
        return carry

    lax.fori_loop(0, BX + 4, clear, 0)
    for l in range(FIELDS):
        for x in (0, 1, BX + 2, BX + 3):
            u[l, x, pl.ds(R0, ROWS), :] = jnp.zeros((ROWS, 128), jnp.float32)

    later, earlier = (jnp.minimum(t + 1, nt - 1), gx, gy), (jnp.maximum(t - 1, 0), gx, gy)
    has_later, has_earlier = t < nt - 1, t > 0
    neighbours = {
        XUP: (gx < nx - 1, (t, jnp.minimum(gx + 1, nx - 1), gy)),
        XDOWN: (gx > 0, (t, jnp.maximum(gx - 1, 0), gy)),
        YUP: (gy < ny - 1, (t, gx, jnp.minimum(gy + 1, ny - 1))),
        YDOWN: (gy > 0, (t, gx, jnp.maximum(gy - 1, 0))),
    }
    opposite = {XUP: XDOWN, XDOWN: XUP, YUP: YDOWN, YDOWN: YUP}
    far_up, far_down = gy == ny // 2 - 1, gy == ny // 2
    far = far_up | far_down

    barrier = pltpu.get_barrier_semaphore()
    partners = jnp.int32(0)
    for present, device in [*neighbours.values(), (has_later, later), (has_earlier, earlier)]:
        @pl.when(present)
        def _(device=device):
            pl.semaphore_signal(barrier, 1, device_id=device, device_id_type=MESH)
        partners = partners + present.astype(jnp.int32)

    lane = lax.broadcasted_iota(jnp.int32, (ROWS, 128), 1)
    half_of = lax.rem(lax.broadcasted_iota(jnp.int32, (ROWS, 128), 0), 2)
    last_lane, first_lane = lane == 127, lane == 0
    bottom, top = first_lane & (half_of == 0), last_lane & (half_of == 1)
    regime = code[0, 0]
    sign_x = 1 - 2 * lax.rem(regime, 2)
    sign_y = 1 - 2 * lax.rem(regime // 2, 2)
    strength = jnp.where(regime // 4 == 1, diffusion_high, diffusion_low).astype(jnp.float32)
    forward_x = jnp.full((ROWS, 128), sign_x, jnp.int32) > 0
    forward_y = jnp.full((ROWS, 128), sign_y, jnp.int32) > 0

    def wind(i):
        pair = [jnp.broadcast_to(profile[pl.ds(i, 1), pl.ds(128 * k, 128)], (ROWS, 128)) for k in range(2)]
        return 0.5 * jnp.where(half_of == 0, pair[0], pair[1])

    wind_x, wind_y = wind(0), wind(1)
    wind_both = 3.0 * (wind_x + wind_y)

    for copy in loads:
        copy.wait()

    def interleave(x, carry):
        for half in range(2):
            u[0, x + X0, pl.ds(R0 + half, BY, stride=2), :] = stage[0, half, x]
            vm[x, pl.ds(half, BY, stride=2), :] = stage[1, half, x]
        return carry

    lax.fori_loop(0, BX, interleave, 0)
    pl.semaphore_wait(barrier, partners)

    def remote(source, target, l, kind, device):
        return pltpu.make_async_remote_copy(
            src_ref=source, dst_ref=target, send_sem=send_sem.at[l, kind], recv_sem=recv_sem.at[l, kind],
            device_id=device, device_id_type=MESH)

    def edge(l, kind):
        device = neighbours[kind][1]
        own, body = pl.ds(R0, ROWS), pl.ds(X0, BX)
        if kind == XUP:
            return remote(u.at[l, pl.ds(BX, 2), own], u.at[l, pl.ds(0, 2), own], l, kind, device)
        if kind == XDOWN:
            return remote(u.at[l, pl.ds(2, 2), own], u.at[l, pl.ds(BX + 2, 2), own], l, kind, device)
        if kind == YUP:
            return remote(u.at[l, body, pl.ds(R1 - 4, 4)], u.at[l, body, pl.ds(R0 - 4, 4)], l, kind, device)
        return remote(u.at[l, body, pl.ds(R0, 4)], u.at[l, body, pl.ds(R1, 4)], l, kind, device)

    def sends(l, kind):
        ok = neighbours[kind][0]
        if l in (1, 4, 7):
            ok = ok & has_earlier
            if kind == YUP:
                ok = ok & (gy != ny // 2 - 1)
            if kind == YDOWN:
                ok = ok & (gy != ny // 2)
        return ok

    def receives(l, kind):
        ok = neighbours[opposite[kind]][0]
        if l in (1, 4, 7):
            ok = ok & has_earlier
            if kind == YUP:
                ok = ok & (gy != ny // 2)
            if kind == YDOWN:
                ok = ok & (gy != ny // 2 - 1)
        return ok

    def start_edges(l):
        for kind in (YUP, YDOWN, XUP, XDOWN):
            @pl.when(sends(l, kind))
            def _(kind=kind):
                edge(l, kind).start()

    def wait_edges(l):
        for kind in (XUP, XDOWN, YUP, YDOWN):
            @pl.when(receives(l, kind))
            def _(kind=kind):
                edge(l, kind).wait_recv()

    def own(l):
        return u.at[l, pl.ds(X0, BX), pl.ds(R0, ROWS)]

    def shift(l):
        return remote(own(l), own(l + 1), l, SHIFT, later)

    def relay(l):
        row = jnp.where(far_up, R1, R0 - 4)
        part = pl.ds(row, 4)
        return remote(u.at[l, pl.ds(X0, BX), part], u.at[l + 1, pl.ds(X0, BX), part], l, FORWARD, later)

    def start_shift(l):
        @pl.when(has_later)
        def _():
            shift(l).start()

    def start_relay(l):
        @pl.when(has_later & far)
        def _():
            relay(l).start()

    def wait_shift(l):
        @pl.when(has_earlier)
        def _():
            shift(l).wait_recv()

    def wait_relay(l):
        @pl.when(has_earlier & far)
        def _():
            relay(l).wait_recv()

    def tendency(l, write):
        def weights(x, carry):
            v = u[l, x, pl.ds(R0 - 8, ROWS + 16), :]
            h[x, pl.ds(R0 - 8, ROWS + 16), :] = 0.75 - 0.5 / (1.0 + v * v)
            return carry

        lax.fori_loop(1, BX + 3, weights, 0)

        def row(x, carry):
            def at(dx, dr):
                return u[l, x + dx, pl.ds(R0 + dr, ROWS), :]

            def weight(dx, dr):
                return h[x + dx, pl.ds(R0 + dr, ROWS), :]

            c, hc = at(0, 0), weight(0, 0)
            xm, xp, ym, yp = at(-1, 0), at(1, 0), at(0, -2), at(0, 2)
            spread = (hc + weight(1, 0)) * (xp - c) + (hc + weight(-1, 0)) * (xm - c)
            spread = spread + ((hc + weight(0, 2)) * (yp - c) + (hc + weight(0, -2)) * (ym - c))
            near_x = jnp.where(forward_x, xm, xp)
            far_x = jnp.where(forward_x, at(-2, 0), at(2, 0))
            near_y = jnp.where(forward_y, ym, yp)
            far_y = jnp.where(forward_y, at(0, -4), at(0, 4))
            carried = wind_x * (far_x - 4.0 * near_x) + wind_y * (far_y - 4.0 * near_y) + wind_both * c
            below = jnp.where(bottom, c, pltpu.roll(jnp.where(last_lane, at(0, -1), c), 1, axis=1))
            above = jnp.where(top, c, pltpu.roll(jnp.where(first_lane, at(0, 1), c), 127, axis=1))
            rate = strength * spread - carried + vm[x - X0] * (below + above - 2.0 * c)
            write(x, c, rate)
            return carry

        lax.fori_loop(X0, X0 + BX, row, 0)

    def initial(x, c, rate):
        c1[x - X0] = A[0] * rate + A[1] * rate + A[2] * rate
        c2[x - X0] = B[0] * rate + B[1] * rate + B[2] * rate

    def to_middle(l):
        def write(x, c, rate):
            u[l, x, pl.ds(R0, ROWS), :] = c + half_step * rate + c1[x - X0]
            p1[x - X0] = rate
        return write

    def to_final(l):
        def write(x, c, rate):
            u[l, x, pl.ds(R0, ROWS), :] = c + half_step * rate + c2[x - X0]
            g0 = p1[x - X0]
            p1[x - X0] = A[0] * g0 + A[1] * rate
            p2[x - X0] = B[0] * g0 + B[1] * rate
        return write

    def finish(x, c, rate):
        c1[x - X0] = p1[x - X0] + A[2] * rate
        c2[x - X0] = p2[x - X0] + B[2] * rate

    def last(x, c, rate):
        u[0, x, pl.ds(R0, ROWS), :] = c + half_step * rate + c2[x - X0]

    def store(k, l, target):
        def split(x, carry):
            for half in range(2):
                out_stage[k, half, x] = u[l, x + X0, pl.ds(R0 + half, BY, stride=2), :]
            return carry

        lax.fori_loop(0, BX, split, 0)
        copies = [
            pltpu.make_async_copy(out_stage.at[k, half], target.at[0, :, :, pl.ds(128 * half, 128)], store_sem.at[k, half])
            for half in range(2)]
        for copy in copies:
            copy.start()
        return copies

    start_shift(0)
    start_edges(0)
    wait_edges(0)
    start_relay(0)
    tendency(0, initial)
    for sweep in range(3):
        end = 3 * sweep
        first, middle = end + 1, end + 2
        wait_shift(end)
        start_edges(first)
        wait_edges(first)
        wait_relay(end)
        tendency(jnp.where(has_earlier, first, 0), to_middle(middle))
        start_edges(middle)
        if sweep < 2:
            wait_edges(middle)
            tendency(middle, to_final(middle + 1))
            start_shift(middle + 1)
            start_edges(middle + 1)
            wait_edges(middle + 1)
            start_relay(middle + 1)
            tendency(middle + 1, finish)
        else:
            stores = store(0, middle, middle_out)
            wait_edges(middle)
            @pl.when(has_later)
            def _():
                shift(0).wait_send()
            for kind in (XUP, XDOWN, YUP, YDOWN):
                @pl.when(sends(0, kind))
                def _(kind=kind):
                    edge(0, kind).wait_send()
            tendency(middle, last)
            stores += store(1, 0, final_out)

    for l in range(FIELDS):
        for kind in (XUP, XDOWN, YUP, YDOWN):
            if l == 0:
                continue
            @pl.when(sends(l, kind))
            def _(l=l, kind=kind):
                edge(l, kind).wait_send()
    for l in (0, 3, 6):
        if l > 0:
            @pl.when(has_later)
            def _(l=l):
                shift(l).wait_send()
        @pl.when(has_later & far)
        def _(l=l):
            relay(l).wait_send()
    for copy in stores:
        copy.wait()


def solution(mesh):
    shape = tuple(mesh.shape[a] for a in ("tm", "gx", "gy"))

    def shards(start_states, wind_code, wind_profile, vertical_mix):
        block = jax.ShapeDtypeStruct(start_states.shape, jnp.float32)
        field = pltpu.VMEM((BX, ROWS, 128), jnp.float32)
        any_space = pl.BlockSpec(memory_space=pl.ANY)
        return pl.pallas_call(
            lambda *refs: kernel(shape, *refs),
            out_shape=(block, block),
            in_specs=[
                any_space,
                pl.BlockSpec(memory_space=pltpu.SMEM),
                pl.BlockSpec(memory_space=pltpu.VMEM),
                any_space,
            ],
            out_specs=(any_space, any_space),
            scratch_shapes=[
                pltpu.VMEM((FIELDS, BX + 4, ROWS + 32, 128), jnp.float32),
                pltpu.VMEM((BX + 4, ROWS + 32, 128), jnp.float32),
                field, field, field, field, field,
                pltpu.VMEM((2, 2, BX, BY, 128), jnp.float32),
                pltpu.VMEM((2, 2, BX, BY, 128), jnp.float32),
                pltpu.SemaphoreType.DMA((2, 2)),
                pltpu.SemaphoreType.DMA((2, 2)),
                pltpu.SemaphoreType.DMA((FIELDS, 6)),
                pltpu.SemaphoreType.DMA((FIELDS, 6)),
            ],
            compiler_params=pltpu.CompilerParams(
                collective_id=0, has_side_effects=True, vmem_limit_bytes=48 * 1024 * 1024),
        )(start_states, wind_code, wind_profile, vertical_mix)

    in_specs = (P("tm", "gx", "gy", None), P("gx", "gy"), P(), P("gx", "gy", None))
    out_specs = (P("tm", "gx", "gy", None), P("tm", "gx", "gy", None))
    return jax.shard_map(shards, mesh=mesh, in_specs=in_specs, out_specs=out_specs, check_vma=False)
```

```python
import jax
import jax.numpy as jnp
from jax import lax
from jax.experimental import pallas as pl
from jax.experimental.pallas import tpu as pltpu
from jax.sharding import PartitionSpec as P

MESH = pl.DeviceIdType.MESH
time_step = 0.5
half_step = 0.25
diffusion_low = 0.04
diffusion_high = 0.1
first_weights = (5.0 / 24.0, 1.0 / 3.0, -1.0 / 24.0)
second_weights = (-1.0 / 24.0, 1.0 / 3.0, 5.0 / 24.0)
A = tuple(time_step * w - (half_step if i == 0 else 0.0) for i, w in enumerate(first_weights))
B = tuple(time_step * w - (half_step if i == 1 else 0.0) for i, w in enumerate(second_weights))

BX = 32
BY = 16
ROWS = 2 * BY
X0 = 2
R0 = 16
R1 = R0 + ROWS
FIELDS = 9
XUP, XDOWN, YUP, YDOWN, SHIFT, REST = range(6)
NEXT = 6


def kernel(shape, start, code, profile, mixing, middle_out, final_out,
           u, h, vm, c1, c2, p1, p2, border, border_c, stage, out_stage, load_sem, store_sem, send_sem, recv_sem):
    nt, nx, ny = shape
    t, gx, gy = (lax.axis_index(a) for a in ("tm", "gx", "gy"))

    loads = []
    for k, source in enumerate((start.at[0], mixing)):
        for half in range(2):
            copy = pltpu.make_async_copy(
                source.at[:, :, pl.ds(128 * half, 128)], stage.at[k, half], load_sem.at[k, half])
            copy.start()
            loads.append(copy)

    def clear(x, carry):
        for l in range(FIELDS):
            u[l, x, pl.ds(R0 - 8, 8), :] = jnp.zeros((8, 128), jnp.float32)
            u[l, x, pl.ds(R1, 8), :] = jnp.zeros((8, 128), jnp.float32)
        return carry

    lax.fori_loop(0, BX + 4, clear, 0)
    for l in range(FIELDS):
        for x in (0, 1, BX + 2, BX + 3):
            u[l, x, pl.ds(R0, ROWS), :] = jnp.zeros((ROWS, 128), jnp.float32)

    later, earlier = (jnp.minimum(t + 1, nt - 1), gx, gy), (jnp.maximum(t - 1, 0), gx, gy)
    has_later, has_earlier = t < nt - 1, t > 0
    neighbours = {
        XUP: (gx < nx - 1, (t, jnp.minimum(gx + 1, nx - 1), gy)),
        XDOWN: (gx > 0, (t, jnp.maximum(gx - 1, 0), gy)),
        YUP: (gy < ny - 1, (t, gx, jnp.minimum(gy + 1, ny - 1))),
        YDOWN: (gy > 0, (t, gx, jnp.maximum(gy - 1, 0))),
    }
    opposite = {XUP: XDOWN, XDOWN: XUP, YUP: YDOWN, YDOWN: YUP}
    far_up, far_down = gy == ny // 2 - 1, gy == ny // 2
    far = far_up | far_down

    def at_time(device, step):
        return (jnp.clip(t + step, 0, nt - 1), device[1], device[2])

    barrier = pltpu.get_barrier_semaphore()
    partners = jnp.int32(0)
    pairs = [(has_later, later), (has_earlier, earlier)]
    for present, device in neighbours.values():
        pairs += [(present, device), (present & has_later, at_time(device, 1)), (present & has_earlier, at_time(device, -1))]
    for present, device in pairs:
        @pl.when(present)
        def _(device=device):
            pl.semaphore_signal(barrier, 1, device_id=device, device_id_type=MESH)
        partners = partners + present.astype(jnp.int32)

    regime = code[0, 0]
    sign_x = 1 - 2 * lax.rem(regime, 2)
    sign_y = 1 - 2 * lax.rem(regime // 2, 2)
    strength = jnp.where(regime // 4 == 1, diffusion_high, diffusion_low).astype(jnp.float32)

    def constants(rows):
        lane = lax.broadcasted_iota(jnp.int32, (rows, 128), 1)
        half_of = lax.rem(lax.broadcasted_iota(jnp.int32, (rows, 128), 0), 2)

        def wind(i):
            pair = [jnp.broadcast_to(profile[pl.ds(i, 1), pl.ds(128 * k, 128)], (rows, 128)) for k in range(2)]
            return 0.5 * jnp.where(half_of == 0, pair[0], pair[1])

        wind_x, wind_y = wind(0), wind(1)
        return (
            lane == 127, lane == 0, (lane == 0) & (half_of == 0), (lane == 127) & (half_of == 1),
            jnp.full((rows, 128), sign_x, jnp.int32) > 0, jnp.full((rows, 128), sign_y, jnp.int32) > 0,
            wind_x, wind_y, 3.0 * (wind_x + wind_y))

    for copy in loads:
        copy.wait()

    def interleave(x, carry):
        for half in range(2):
            u[0, x + X0, pl.ds(R0 + half, BY, stride=2), :] = stage[0, half, x]
            vm[x, pl.ds(half, BY, stride=2), :] = stage[1, half, x]
        return carry

    lax.fori_loop(0, BX, interleave, 0)
    pl.semaphore_wait(barrier, partners)

    def remote(source, target, l, kind, device):
        return pltpu.make_async_remote_copy(
            src_ref=source, dst_ref=target, send_sem=send_sem.at[l, kind], recv_sem=recv_sem.at[l, kind],
            device_id=device, device_id_type=MESH)

    def edge(l, kind, step=0, source=None):
        device = at_time(neighbours[kind][1], step)
        m = l + step
        own, body = pl.ds(R0, ROWS), pl.ds(X0, BX)
        if kind == XUP:
            source, target = u.at[l, pl.ds(BX, 2), own], u.at[m, pl.ds(0, 2), own]
        elif kind == XDOWN:
            source, target = u.at[l, pl.ds(2, 2), own], u.at[m, pl.ds(BX + 2, 2), own]
        elif kind == YUP:
            source, target = source or u.at[l, body, pl.ds(R1 - 4, 4)], u.at[m, body, pl.ds(R0 - 4, 4)]
        else:
            source, target = source or u.at[l, body, pl.ds(R0, 4)], u.at[m, body, pl.ds(R1, 4)]
        return remote(source, target, l, kind + NEXT * step, device)

    def is_far(kind, receiving=False):
        if kind in (XUP, XDOWN):
            return None
        return far_up if (kind == YUP) != receiving else far_down

    def each_edge(action, l, kinds=(YUP, YDOWN, XUP, XDOWN), step=0, far_ones=None):
        receiving = action == "wait_recv"
        for kind in kinds:
            ok = neighbours[opposite[kind] if receiving else kind][0]
            if step:
                ok = ok & (has_earlier if receiving else has_later)
            crossing = is_far(kind, receiving)
            if far_ones is not None:
                if crossing is None:
                    continue
                ok = ok & (crossing if far_ones else ~crossing)

            @pl.when(ok)
            def _(kind=kind):
                source = border.at[l // 3] if far_ones and l % 3 == 2 else None
                getattr(edge(l, kind, step, source), action)()

    def shift(l, kind):
        if kind == SHIFT:
            rows = pl.ds(jnp.where(far_up, R1 - 8, R0), 8)
        else:
            rows = pl.ds(jnp.where(far_up, R0, R0 + 8), ROWS - 8)
        body = pl.ds(X0, BX)
        return remote(u.at[l, body, rows], u.at[l + 1, body, rows], l, kind, later)

    def each_shift(action, l, kind):
        @pl.when(has_earlier if action == "wait_recv" else has_later)
        def _():
            getattr(shift(l, kind), action)()

    def tendency(l, write, r0=R0, rows=ROWS, parts=((X0, X0 + BX, None),), unroll=4):
        last_lane, first_lane, bottom, top, forward_x, forward_y, wind_x, wind_y, wind_both = constants(rows)

        def weights(x, carry):
            v = u[l, x, pl.ds(r0 - 2, rows + 4), :]
            h[x, pl.ds(r0 - 2, rows + 4), :] = 0.75 - 0.5 / (1.0 + v * v)
            return carry

        lax.fori_loop(1, BX + 3, weights, 0, unroll=2)

        def row(x, carry):
            def at(dx, dr):
                return u[l, x + dx, pl.ds(r0 + dr, rows), :]

            def weight(dx, dr):
                return h[x + dx, pl.ds(r0 + dr, rows), :]

            c, hc = at(0, 0), weight(0, 0)
            xm, xp, ym, yp = at(-1, 0), at(1, 0), at(0, -2), at(0, 2)
            spread = (hc + weight(1, 0)) * (xp - c) + (hc + weight(-1, 0)) * (xm - c)
            spread = spread + ((hc + weight(0, 2)) * (yp - c) + (hc + weight(0, -2)) * (ym - c))
            near_x = jnp.where(forward_x, xm, xp)
            far_x = jnp.where(forward_x, at(-2, 0), at(2, 0))
            near_y = jnp.where(forward_y, ym, yp)
            far_y = jnp.where(forward_y, at(0, -4), at(0, 4))
            carried = wind_x * (far_x - 4.0 * near_x) + wind_y * (far_y - 4.0 * near_y) + wind_both * c
            below = jnp.where(bottom, c, pltpu.roll(jnp.where(last_lane, at(0, -1), c), 1, axis=1))
            above = jnp.where(top, c, pltpu.roll(jnp.where(first_lane, at(0, 1), c), 127, axis=1))
            rate = strength * spread - carried + vm[x - X0, pl.ds(r0 - R0, rows), :] * (below + above - 2.0 * c)
            write(x, c, rate)
            return carry

        for begin, end, after in parts:
            lax.fori_loop(begin, end, row, 0, unroll=min(unroll, end - begin))
            if after is not None:
                after()

    def initial(x, c, rate):
        c1[x - X0] = A[0] * rate + A[1] * rate + A[2] * rate
        c2[x - X0] = B[0] * rate + B[1] * rate + B[2] * rate

    def to_middle(l):
        def write(x, c, rate):
            u[l, x, pl.ds(R0, ROWS), :] = c + half_step * rate + c1[x - X0]
            p1[x - X0] = rate
        return write

    def to_final(l):
        def write(x, c, rate):
            u[l, x, pl.ds(R0, ROWS), :] = c + half_step * rate + c2[x - X0]
            g0 = p1[x - X0]
            p1[x - X0] = A[0] * g0 + A[1] * rate
            p2[x - X0] = B[0] * g0 + B[1] * rate
        return write

    def finish(x, c, rate):
        c1[x - X0] = p1[x - X0] + A[2] * rate
        c2[x - X0] = p2[x - X0] + B[2] * rate

    def last(x, c, rate):
        u[0, x, pl.ds(R0, ROWS), :] = c + half_step * rate + c2[x - X0]

    def store(k, l, target):
        def split(x, carry):
            for half in range(2):
                out_stage[k, half, x] = u[l, x + X0, pl.ds(R0 + half, BY, stride=2), :]
            return carry

        lax.fori_loop(0, BX, split, 0)
        copies = [
            pltpu.make_async_copy(out_stage.at[k, half], target.at[0, :, :, pl.ds(128 * half, 128)], store_sem.at[k, half])
            for half in range(2)]
        for copy in copies:
            copy.start()
        return copies

    def border_first(sweep, end, source):
        def run(r0, kind):
            rows = pl.ds(r0 - R0, 4)

            def slopes(x, c, rate):
                if sweep == 0:
                    border_c[x - X0] = A[0] * rate + A[1] * rate + A[2] * rate
                else:
                    border_c[x - X0] = p1[x - X0, rows, :] + A[2] * rate

            def state(x, c, rate):
                border[sweep, x - X0] = c + half_step * rate + border_c[x - X0]

            each_edge("wait_recv", end, (opposite[kind],))
            tendency(end, slopes, r0, 4, unroll=8)
            each_shift("wait_recv", end, SHIFT)
            each_edge("wait_recv", end, (XUP, XDOWN, opposite[kind]), step=1)
            tendency(source, state, r0, 4, unroll=8)

        each_edge("wait_recv", end, (XUP, XDOWN))

        @pl.when(far_up)
        def _():
            run(R1 - 4, YUP)

        @pl.when(far_down)
        def _():
            run(R0, YDOWN)

    stores = []
    for sweep in range(3):
        end, middle = 3 * sweep, 3 * sweep + 2
        source = jnp.where(has_earlier, end + 1, 0)
        each_edge("start", end, (YUP, YDOWN), far_ones=True)
        each_edge("start", end, (YUP, YDOWN), step=1, far_ones=True)
        each_edge("start", end, (XUP, XDOWN))
        each_edge("start", end, (YUP, YDOWN), far_ones=False)
        each_shift("start", end, SHIFT)
        each_edge("start", end, (XUP, XDOWN), step=1)
        each_edge("start", end, (YUP, YDOWN), step=1, far_ones=False)
        each_shift("start", end, REST)
        border_first(sweep, end, source)
        each_edge("start", middle, (YUP, YDOWN), far_ones=True)
        each_edge("wait_recv", end, (YUP, YDOWN), far_ones=False)
        tendency(end, initial if sweep == 0 else finish)

        @pl.when(~far)
        def _():
            each_shift("wait_recv", end, SHIFT)
            each_edge("wait_recv", end, (XUP, XDOWN), step=1)

        each_edge("wait_recv", end, (YUP, YDOWN), step=1, far_ones=False)
        each_shift("wait_recv", end, REST)

        def send_x():
            each_edge("start", middle, (XUP, XDOWN))

        tendency(source, to_middle(middle), parts=(
            (X0, X0 + 2, None), (X0 + BX - 2, X0 + BX, send_x), (X0 + 2, X0 + BX - 2, None)))
        each_edge("start", middle, (YUP, YDOWN), far_ones=False)
        if sweep == 2:
            stores += store(0, middle, middle_out)
        each_edge("wait_recv", middle)
        if sweep < 2:
            tendency(middle, to_final(middle + 1))
        else:
            each_edge("wait_send", 0)
            each_edge("wait_send", 0, step=1)
            each_shift("wait_send", 0, SHIFT)
            each_shift("wait_send", 0, REST)
            tendency(middle, last)
            stores += store(1, 0, final_out)

    for end in (0, 3, 6):
        if end:
            each_edge("wait_send", end)
            each_edge("wait_send", end, step=1)
            each_shift("wait_send", end, SHIFT)
            each_shift("wait_send", end, REST)
        each_edge("wait_send", end + 2, (XUP, XDOWN))
        each_edge("wait_send", end + 2, (YUP, YDOWN), far_ones=False)
        each_edge("wait_send", end + 2, (YUP, YDOWN), far_ones=True)
    for copy in stores:
        copy.wait()


def solution(mesh):
    shape = tuple(mesh.shape[a] for a in ("tm", "gx", "gy"))

    def shards(start_states, wind_code, wind_profile, vertical_mix):
        block = jax.ShapeDtypeStruct(start_states.shape, jnp.float32)
        field = pltpu.VMEM((BX, ROWS, 128), jnp.float32)
        any_space = pl.BlockSpec(memory_space=pl.ANY)
        return pl.pallas_call(
            lambda *refs: kernel(shape, *refs),
            out_shape=(block, block),
            in_specs=[
                any_space,
                pl.BlockSpec(memory_space=pltpu.SMEM),
                pl.BlockSpec(memory_space=pltpu.VMEM),
                any_space,
            ],
            out_specs=(any_space, any_space),
            scratch_shapes=[
                pltpu.VMEM((FIELDS, BX + 4, ROWS + 32, 128), jnp.float32),
                pltpu.VMEM((BX + 4, ROWS + 32, 128), jnp.float32),
                field, field, field, field, field,
                pltpu.VMEM((3, BX, 4, 128), jnp.float32),
                pltpu.VMEM((BX, 4, 128), jnp.float32),
                pltpu.VMEM((2, 2, BX, BY, 128), jnp.float32),
                pltpu.VMEM((2, 2, BX, BY, 128), jnp.float32),
                pltpu.SemaphoreType.DMA((2, 2)),
                pltpu.SemaphoreType.DMA((2, 2)),
                pltpu.SemaphoreType.DMA((FIELDS, 2 * NEXT)),
                pltpu.SemaphoreType.DMA((FIELDS, 2 * NEXT)),
            ],
            compiler_params=pltpu.CompilerParams(
                collective_id=0, has_side_effects=True),
        )(start_states, wind_code, wind_profile, vertical_mix)

    in_specs = (P("tm", "gx", "gy", None), P("gx", "gy"), P(), P("gx", "gy", None))
    out_specs = (P("tm", "gx", "gy", None), P("tm", "gx", "gy", None))
    return jax.shard_map(shards, mesh=mesh, in_specs=in_specs, out_specs=out_specs, check_vma=False)
```

```python
import jax
import jax.numpy as jnp
from jax import lax
from jax.experimental import pallas as pl
from jax.experimental.pallas import tpu as pltpu
from jax.sharding import PartitionSpec as P

MESH = pl.DeviceIdType.MESH
time_step = 0.5
half_step = 0.25
diffusion_low = 0.04
diffusion_high = 0.1
first_weights = (5.0 / 24.0, 1.0 / 3.0, -1.0 / 24.0)
second_weights = (-1.0 / 24.0, 1.0 / 3.0, 5.0 / 24.0)
A = tuple(time_step * w - (half_step if i == 0 else 0.0) for i, w in enumerate(first_weights))
B = tuple(time_step * w - (half_step if i == 1 else 0.0) for i, w in enumerate(second_weights))

BX = 32
BY = 16
ROWS = 2 * BY
X0 = 2
R0 = 16
R1 = R0 + ROWS
FIELDS = 9
XUP, XDOWN, YUP, YDOWN, STRIP, LOW, HIGH, REST = range(8)
NEXT = 8


def kernel(shape, start, code, wind_profile, mixing, middle_out, final_out,
           u, h, vm, c1, c2, p1, p2, border, border_c, stage, profile, profile_sem, load_sem, send_sem, recv_sem):
    nt, nx, ny = shape
    t, gx, gy = (lax.axis_index(a) for a in ("tm", "gx", "gy"))

    loads = [pltpu.make_async_copy(wind_profile, profile, profile_sem)]
    loads[0].start()
    for k, source in enumerate((start.at[0], mixing)):
        for half in range(2):
            copy = pltpu.make_async_copy(
                source.at[:, :, pl.ds(128 * half, 128)], stage.at[k, half], load_sem.at[k, half])
            copy.start()
            loads.append(copy)

    def clear(x, carry):
        for l in range(FIELDS):
            u[l, x, pl.ds(R0 - 8, 8), :] = jnp.zeros((8, 128), jnp.float32)
            u[l, x, pl.ds(R1, 8), :] = jnp.zeros((8, 128), jnp.float32)
        return carry

    lax.fori_loop(0, BX + 4, clear, 0)
    for l in range(FIELDS):
        for x in (0, 1, BX + 2, BX + 3):
            u[l, x, pl.ds(R0, ROWS), :] = jnp.zeros((ROWS, 128), jnp.float32)

    later, earlier = (jnp.minimum(t + 1, nt - 1), gx, gy), (jnp.maximum(t - 1, 0), gx, gy)
    has_later, has_earlier = t < nt - 1, t > 0
    neighbours = {
        XUP: (gx < nx - 1, (t, jnp.minimum(gx + 1, nx - 1), gy)),
        XDOWN: (gx > 0, (t, jnp.maximum(gx - 1, 0), gy)),
        YUP: (gy < ny - 1, (t, gx, jnp.minimum(gy + 1, ny - 1))),
        YDOWN: (gy > 0, (t, gx, jnp.maximum(gy - 1, 0))),
    }
    opposite = {XUP: XDOWN, XDOWN: XUP, YUP: YDOWN, YDOWN: YUP}
    far_up, far_down = gy == ny // 2 - 1, gy == ny // 2
    far = far_up | far_down

    def at_time(device, step):
        return (jnp.clip(t + step, 0, nt - 1), device[1], device[2])

    barrier = pltpu.get_barrier_semaphore()
    partners = jnp.int32(0)
    pairs = [(has_later, later), (has_earlier, earlier)]
    for present, device in neighbours.values():
        pairs += [(present, device), (present & has_later, at_time(device, 1)), (present & has_earlier, at_time(device, -1))]
    for present, device in pairs:
        @pl.when(present)
        def _(device=device):
            pl.semaphore_signal(barrier, 1, device_id=device, device_id_type=MESH)
        partners = partners + present.astype(jnp.int32)

    regime = code[0, 0]
    sign_x = 1 - 2 * lax.rem(regime, 2)
    sign_y = 1 - 2 * lax.rem(regime // 2, 2)
    strength = jnp.where(regime // 4 == 1, diffusion_high, diffusion_low).astype(jnp.float32)

    def constants(rows):
        lane = lax.broadcasted_iota(jnp.int32, (rows, 128), 1)
        half_of = lax.rem(lax.broadcasted_iota(jnp.int32, (rows, 128), 0), 2)

        def wind(i):
            pair = [jnp.broadcast_to(profile[pl.ds(i, 1), pl.ds(128 * k, 128)], (rows, 128)) for k in range(2)]
            return 0.5 * jnp.where(half_of == 0, pair[0], pair[1])

        wind_x, wind_y = wind(0), wind(1)
        return (
            lane == 127, lane == 0, (lane == 0) & (half_of == 0), (lane == 127) & (half_of == 1),
            jnp.full((rows, 128), sign_x, jnp.int32) > 0, jnp.full((rows, 128), sign_y, jnp.int32) > 0,
            wind_x, wind_y, 3.0 * (wind_x + wind_y))

    for copy in loads:
        copy.wait()

    def interleave(x, carry):
        for half in range(2):
            u[0, x + X0, pl.ds(R0 + half, BY, stride=2), :] = stage[0, half, x]
            vm[x, pl.ds(half, BY, stride=2), :] = stage[1, half, x]
        return carry

    lax.fori_loop(0, BX, interleave, 0)
    pl.semaphore_wait(barrier, partners)

    def remote(source, target, l, kind, device):
        return pltpu.make_async_remote_copy(
            src_ref=source, dst_ref=target, send_sem=send_sem.at[l, kind], recv_sem=recv_sem.at[l, kind],
            device_id=device, device_id_type=MESH)

    def edge(l, kind, step=0, source=None):
        device = at_time(neighbours[kind][1], step)
        m = l + step
        own, body = pl.ds(R0, ROWS), pl.ds(X0, BX)
        if kind == XUP:
            source, target = u.at[l, pl.ds(BX, 2), own], u.at[m, pl.ds(0, 2), own]
        elif kind == XDOWN:
            source, target = u.at[l, pl.ds(2, 2), own], u.at[m, pl.ds(BX + 2, 2), own]
        elif kind == YUP:
            source, target = source or u.at[l, body, pl.ds(R1 - 4, 4)], u.at[m, body, pl.ds(R0 - 4, 4)]
        else:
            source, target = source or u.at[l, body, pl.ds(R0, 4)], u.at[m, body, pl.ds(R1, 4)]
        return remote(source, target, l, kind + NEXT * step, device)

    def is_far(kind, receiving=False):
        if kind in (XUP, XDOWN):
            return None
        return far_up if (kind == YUP) != receiving else far_down

    def each_edge(action, l, kinds=(YUP, YDOWN, XUP, XDOWN), step=0, far_ones=None):
        receiving = action == "wait_recv"
        for kind in kinds:
            ok = neighbours[opposite[kind] if receiving else kind][0]
            if step:
                ok = ok & (has_earlier if receiving else has_later)
            crossing = is_far(kind, receiving)
            if far_ones is not None:
                if crossing is None:
                    continue
                ok = ok & (crossing if far_ones else ~crossing)

            @pl.when(ok)
            def _(kind=kind):
                source = border.at[l // 3] if far_ones and l % 3 == 2 else None
                getattr(edge(l, kind, step, source), action)()

    def shift(l, kind):
        if kind == STRIP:
            rows, body = pl.ds(jnp.where(far_up, R1 - 8, R0), 8), pl.ds(X0, BX)
        else:
            rows = pl.ds(jnp.where(far_up, R0, R0 + 8), ROWS - 8)
            body = {LOW: pl.ds(X0, 4), HIGH: pl.ds(X0 + BX - 4, 4), REST: pl.ds(X0 + 4, BX - 8)}[kind]
        return remote(u.at[l, body, rows], u.at[l + 1, body, rows], l, kind, later)

    def each_shift(action, l, kind):
        @pl.when(has_earlier if action == "wait_recv" else has_later)
        def _():
            getattr(shift(l, kind), action)()

    def tendency(l, write, r0=R0, rows=ROWS, begin=X0, end=X0 + BX, unroll=4):
        last_lane, first_lane, bottom, top, forward_x, forward_y, wind_x, wind_y, wind_both = constants(rows)

        def weights(x, carry):
            v = u[l, x, pl.ds(r0 - 2, rows + 4), :]
            h[x, pl.ds(r0 - 2, rows + 4), :] = 0.75 - 0.5 / (1.0 + v * v)
            return carry

        def row(x, carry):
            def at(dx, dr):
                return u[l, x + dx, pl.ds(r0 + dr, rows), :]

            def weight(dx, dr):
                return h[x + dx, pl.ds(r0 + dr, rows), :]

            c, hc = at(0, 0), weight(0, 0)
            xm, xp, ym, yp = at(-1, 0), at(1, 0), at(0, -2), at(0, 2)
            spread = (hc + weight(1, 0)) * (xp - c) + (hc + weight(-1, 0)) * (xm - c)
            spread = spread + ((hc + weight(0, 2)) * (yp - c) + (hc + weight(0, -2)) * (ym - c))
            near_x = jnp.where(forward_x, xm, xp)
            far_x = jnp.where(forward_x, at(-2, 0), at(2, 0))
            near_y = jnp.where(forward_y, ym, yp)
            far_y = jnp.where(forward_y, at(0, -4), at(0, 4))
            carried = wind_x * (far_x - 4.0 * near_x) + wind_y * (far_y - 4.0 * near_y) + wind_both * c
            below = jnp.where(bottom, c, pltpu.roll(jnp.where(last_lane, at(0, -1), c), 1, axis=1))
            above = jnp.where(top, c, pltpu.roll(jnp.where(first_lane, at(0, 1), c), 127, axis=1))
            rate = strength * spread - carried + vm[x - X0, pl.ds(r0 - R0, rows), :] * (below + above - 2.0 * c)
            write(x, c, rate)
            return carry

        if begin is None:
            for x in (1, 2, 3, 4, BX - 1, BX, BX + 1, BX + 2):
                weights(x, 0)
            for x in (X0, X0 + 1, BX, BX + 1):
                row(x, 0)
        else:
            lax.fori_loop(begin - 1, end + 1, weights, 0, unroll=2)
            lax.fori_loop(begin, end, row, 0, unroll=unroll)

    def initial(x, c, rate):
        c1[x - X0] = A[0] * rate + A[1] * rate + A[2] * rate
        c2[x - X0] = B[0] * rate + B[1] * rate + B[2] * rate

    def to_middle(l, out):
        def write(x, c, rate):
            state = c + half_step * rate + c1[x - X0]
            u[l, x, pl.ds(R0, ROWS), :] = state
            if out is None:
                p1[x - X0] = rate
            else:
                out[x - X0] = state
        return write

    def to_final(l, r0, rows):
        own = pl.ds(r0 - R0, rows)

        def write(x, c, rate):
            u[l, x, pl.ds(r0, rows), :] = c + half_step * rate + c2[x - X0, own, :]
            g0 = p1[x - X0, own, :]
            p1[x - X0, own, :] = A[0] * g0 + A[1] * rate
            p2[x - X0, own, :] = B[0] * g0 + B[1] * rate
        return write

    def finish(x, c, rate):
        c1[x - X0] = p1[x - X0] + A[2] * rate
        c2[x - X0] = p2[x - X0] + B[2] * rate

    def last(r0, rows):
        own = pl.ds(r0 - R0, rows)

        def write(x, c, rate):
            final_out[x - X0, own, :] = c + half_step * rate + c2[x - X0, own, :]
        return write

    def copy_start():
        def body(x, carry):
            rows = pl.ds(R0 - 8, ROWS + 16)
            for l in (1, 4, 7):
                u[l, x, rows, :] = u[0, x, rows, :]
            return carry

        @pl.when(~has_earlier)
        def _():
            lax.fori_loop(0, BX + 4, body, 0, unroll=2)

    def border_first(sweep, end):
        def run(r0, kind):
            rows = pl.ds(r0 - R0, 4)

            def slopes(x, c, rate):
                if sweep == 0:
                    border_c[x - X0] = A[0] * rate + A[1] * rate + A[2] * rate
                else:
                    border_c[x - X0] = p1[x - X0, rows, :] + A[2] * rate

            def state(x, c, rate):
                border[sweep, x - X0] = c + half_step * rate + border_c[x - X0]

            each_edge("wait_recv", end, (opposite[kind],))
            tendency(end, slopes, r0, 4, unroll=8)
            if sweep == 0:
                copy_start()
            each_shift("wait_recv", end, STRIP)
            each_edge("wait_recv", end, (XUP, XDOWN, opposite[kind]), step=1)
            tendency(end + 1, state, r0, 4, unroll=8)

        each_edge("wait_recv", end, (YUP, YDOWN), far_ones=False)

        @pl.when(far_up)
        def _():
            run(R1 - 4, YUP)

        @pl.when(far_down)
        def _():
            run(R0, YDOWN)

        if sweep == 0:
            @pl.when(~far)
            def _():
                copy_start()

    for sweep in range(3):
        end, first, middle = 3 * sweep, 3 * sweep + 1, 3 * sweep + 2
        each_edge("start", end, (YUP, YDOWN), far_ones=True)
        each_edge("start", end, (YUP, YDOWN), step=1, far_ones=True)
        each_edge("start", end, (XUP, XDOWN), step=1)
        each_edge("start", end, (XUP, XDOWN))
        each_edge("start", end, (YUP, YDOWN), far_ones=False)
        each_shift("start", end, STRIP)
        each_edge("start", end, (YUP, YDOWN), step=1, far_ones=False)
        each_edge("wait_recv", end, (XUP, XDOWN))
        for kind in (LOW, HIGH, REST):
            each_shift("start", end, kind)
        border_first(sweep, end)
        each_edge("start", middle, (YUP, YDOWN), far_ones=True)
        tendency(end, initial if sweep == 0 else finish)

        @pl.when(~far)
        def _():
            each_shift("wait_recv", end, STRIP)
            each_edge("wait_recv", end, (XUP, XDOWN), step=1)

        each_edge("wait_recv", end, (YUP, YDOWN), step=1, far_ones=False)
        each_shift("wait_recv", end, LOW)
        each_shift("wait_recv", end, HIGH)
        write = to_middle(middle, middle_out if sweep == 2 else None)
        tendency(first, write, begin=None)
        each_edge("start", middle, (XUP, XDOWN))
        each_shift("wait_recv", end, REST)
        tendency(first, write, begin=X0 + 2, end=X0 + BX - 2)
        each_edge("start", middle, (YUP, YDOWN), far_ones=False)
        each_edge("wait_recv", middle, (XUP, XDOWN))
        each_edge("wait_recv", middle, (YUP, YDOWN), far_ones=False)

        def part(r0, rows, unroll=4):
            write = to_final(middle + 1, r0, rows) if sweep < 2 else last(r0, rows)
            tendency(middle, write, r0, rows, unroll=unroll)

        @pl.when(~far)
        def _():
            part(R0, ROWS)

        @pl.when(far_up)
        def _():
            part(R0, ROWS - 4)
            each_edge("wait_recv", middle, (YDOWN,))
            part(R1 - 4, 4, 8)

        @pl.when(far_down)
        def _():
            part(R0 + 4, ROWS - 4)
            each_edge("wait_recv", middle, (YUP,))
            part(R0, 4, 8)

    for end in (0, 3, 6):
        each_edge("wait_send", end)
        each_edge("wait_send", end, step=1)
        for kind in (STRIP, LOW, HIGH, REST):
            each_shift("wait_send", end, kind)
        each_edge("wait_send", end + 2, (XUP, XDOWN))
        each_edge("wait_send", end + 2, (YUP, YDOWN), far_ones=False)
        each_edge("wait_send", end + 2, (YUP, YDOWN), far_ones=True)


def unpack(middle, final, middle_out, final_out):
    def body(x, carry):
        for source, target in ((middle, middle_out), (final, final_out)):
            for half in range(2):
                target[0, x, :, pl.ds(128 * half, 128)] = source[x, pl.ds(half, BY, stride=2), :]
        return carry

    lax.fori_loop(0, middle.shape[0], body, 0, unroll=4)


def solution(mesh):
    shape = tuple(mesh.shape[a] for a in ("tm", "gx", "gy"))

    def shards(start_states, wind_code, wind_profile, vertical_mix):
        block = jax.ShapeDtypeStruct(start_states.shape, jnp.float32)
        packed = jax.ShapeDtypeStruct((BX, ROWS, 128), jnp.float32)
        field = pltpu.VMEM(packed.shape, jnp.float32)
        any_space, vmem = pl.BlockSpec(memory_space=pl.ANY), pl.BlockSpec(memory_space=pltpu.VMEM)
        middle, final = pl.pallas_call(
            lambda *refs: kernel(shape, *refs),
            out_shape=(packed, packed),
            in_specs=[any_space, pl.BlockSpec(memory_space=pltpu.SMEM), any_space, any_space],
            out_specs=(vmem, vmem),
            scratch_shapes=[
                pltpu.VMEM((FIELDS, BX + 4, ROWS + 32, 128), jnp.float32),
                pltpu.VMEM((BX + 4, ROWS + 32, 128), jnp.float32),
                field, field, field, field, field,
                pltpu.VMEM((3, BX, 4, 128), jnp.float32),
                pltpu.VMEM((BX, 4, 128), jnp.float32),
                pltpu.VMEM((2, 2, BX, BY, 128), jnp.float32),
                pltpu.VMEM((2, 256), jnp.float32),
                pltpu.SemaphoreType.DMA,
                pltpu.SemaphoreType.DMA((2, 2)),
                pltpu.SemaphoreType.DMA((FIELDS, NEXT + 4)),
                pltpu.SemaphoreType.DMA((FIELDS, NEXT + 4)),
            ],
            compiler_params=pltpu.CompilerParams(collective_id=0, has_side_effects=True, vmem_limit_bytes=54000 * 1024),
        )(start_states, wind_code, pltpu.with_memory_space_constraint(wind_profile, pltpu.HBM), vertical_mix)
        return pl.pallas_call(
            unpack,
            out_shape=(block, block),
            in_specs=[vmem, vmem],
            out_specs=(vmem, vmem),
            compiler_params=pltpu.CompilerParams(vmem_limit_bytes=8 * 1024 * 1024),
        )(middle, final)

    in_specs = (P("tm", "gx", "gy", None), P("gx", "gy"), P(), P("gx", "gy", None))
    out_specs = (P("tm", "gx", "gy", None), P("tm", "gx", "gy", None))
    return jax.shard_map(shards, mesh=mesh, in_specs=in_specs, out_specs=out_specs, check_vma=False)
```

```python
import jax
import jax.numpy as jnp
from jax import lax
from jax.experimental import pallas as pl
from jax.experimental.pallas import tpu as pltpu
from jax.sharding import PartitionSpec as P

MESH = pl.DeviceIdType.MESH
time_step = 0.5
half_step = 0.25
diffusion_low = 0.04
diffusion_high = 0.1
first_weights = (5.0 / 24.0, 1.0 / 3.0, -1.0 / 24.0)
second_weights = (-1.0 / 24.0, 1.0 / 3.0, 5.0 / 24.0)
A = tuple(time_step * w - (half_step if i == 0 else 0.0) for i, w in enumerate(first_weights))
B = tuple(time_step * w - (half_step if i == 1 else 0.0) for i, w in enumerate(second_weights))

BX = 32
BY = 16
ROWS = 2 * BY
X0 = 2
R0 = 16
R1 = R0 + ROWS
FIELDS = 9
XUP, XDOWN, YUP, YDOWN, STRIP, LOW, HIGH, REST = range(8)
NEXT = 8


def kernel(shape, start, code, wind_profile, mixing, middle_out, final_out,
           u, h, vm, c1, c2, p1, p2, border, border_c, stage, profile, profile_sem, load_sem, send_sem, recv_sem):
    nt, nx, ny = shape
    t, gx, gy = (lax.axis_index(a) for a in ("tm", "gx", "gy"))

    loads = [pltpu.make_async_copy(wind_profile, profile, profile_sem)]
    loads[0].start()
    for k, source in enumerate((start.at[0], mixing)):
        for half in range(2):
            copy = pltpu.make_async_copy(
                source.at[:, :, pl.ds(128 * half, 128)], stage.at[k, half], load_sem.at[k, half])
            copy.start()
            loads.append(copy)

    def clear(x, carry):
        for l in range(FIELDS):
            u[l, x, pl.ds(R0 - 8, 8), :] = jnp.zeros((8, 128), jnp.float32)
            u[l, x, pl.ds(R1, 8), :] = jnp.zeros((8, 128), jnp.float32)
        return carry

    lax.fori_loop(0, BX + 4, clear, 0)
    for l in range(FIELDS):
        for x in (0, 1, BX + 2, BX + 3):
            u[l, x, pl.ds(R0, ROWS), :] = jnp.zeros((ROWS, 128), jnp.float32)

    later, earlier = (jnp.minimum(t + 1, nt - 1), gx, gy), (jnp.maximum(t - 1, 0), gx, gy)
    has_later, has_earlier = t < nt - 1, t > 0
    neighbours = {
        XUP: (gx < nx - 1, (t, jnp.minimum(gx + 1, nx - 1), gy)),
        XDOWN: (gx > 0, (t, jnp.maximum(gx - 1, 0), gy)),
        YUP: (gy < ny - 1, (t, gx, jnp.minimum(gy + 1, ny - 1))),
        YDOWN: (gy > 0, (t, gx, jnp.maximum(gy - 1, 0))),
    }
    opposite = {XUP: XDOWN, XDOWN: XUP, YUP: YDOWN, YDOWN: YUP}
    far_up, far_down = gy == ny // 2 - 1, gy == ny // 2
    far = far_up | far_down

    def at_time(device, step):
        return (jnp.clip(t + step, 0, nt - 1), device[1], device[2])

    barrier = pltpu.get_barrier_semaphore()
    partners = jnp.int32(0)
    pairs = [(has_later, later), (has_earlier, earlier)]
    for present, device in neighbours.values():
        pairs += [(present, device), (present & has_later, at_time(device, 1)), (present & has_earlier, at_time(device, -1))]
    for present, device in pairs:
        @pl.when(present)
        def _(device=device):
            pl.semaphore_signal(barrier, 1, device_id=device, device_id_type=MESH)
        partners = partners + present.astype(jnp.int32)

    regime = code[0, 0]
    sign_x = 1 - 2 * lax.rem(regime, 2)
    sign_y = 1 - 2 * lax.rem(regime // 2, 2)
    strength = jnp.where(regime // 4 == 1, diffusion_high, diffusion_low).astype(jnp.float32)

    def constants(rows):
        lane = lax.broadcasted_iota(jnp.int32, (rows, 128), 1)
        half_of = lax.rem(lax.broadcasted_iota(jnp.int32, (rows, 128), 0), 2)

        def wind(i):
            pair = [jnp.broadcast_to(profile[pl.ds(i, 1), pl.ds(128 * k, 128)], (rows, 128)) for k in range(2)]
            return 0.5 * jnp.where(half_of == 0, pair[0], pair[1])

        wind_x, wind_y = wind(0), wind(1)
        return (
            lane == 127, lane == 0, (lane == 0) & (half_of == 0), (lane == 127) & (half_of == 1),
            jnp.full((rows, 128), sign_x, jnp.int32) > 0, jnp.full((rows, 128), sign_y, jnp.int32) > 0,
            wind_x, wind_y, 3.0 * (wind_x + wind_y))

    for copy in loads:
        copy.wait()

    def interleave(x, carry):
        for half in range(2):
            u[0, x + X0, pl.ds(R0 + half, BY, stride=2), :] = stage[0, half, x]
            vm[x, pl.ds(half, BY, stride=2), :] = stage[1, half, x]
        return carry

    lax.fori_loop(0, BX, interleave, 0)
    pl.semaphore_wait(barrier, partners)

    def remote(source, target, l, kind, device):
        return pltpu.make_async_remote_copy(
            src_ref=source, dst_ref=target, send_sem=send_sem.at[l, kind], recv_sem=recv_sem.at[l, kind],
            device_id=device, device_id_type=MESH)

    def edge(l, kind, step=0, source=None):
        device = at_time(neighbours[kind][1], step)
        m = l + step
        own, body = pl.ds(R0, ROWS), pl.ds(X0, BX)
        if kind == XUP:
            source, target = u.at[l, pl.ds(BX, 2), own], u.at[m, pl.ds(0, 2), own]
        elif kind == XDOWN:
            source, target = u.at[l, pl.ds(2, 2), own], u.at[m, pl.ds(BX + 2, 2), own]
        elif kind == YUP:
            source, target = source or u.at[l, body, pl.ds(R1 - 4, 4)], u.at[m, body, pl.ds(R0 - 4, 4)]
        else:
            source, target = source or u.at[l, body, pl.ds(R0, 4)], u.at[m, body, pl.ds(R1, 4)]
        return remote(source, target, l, kind + NEXT * step, device)

    def is_far(kind, receiving=False):
        if kind in (XUP, XDOWN):
            return None
        return far_up if (kind == YUP) != receiving else far_down

    def each_edge(action, l, kinds=(YUP, YDOWN, XUP, XDOWN), step=0, far_ones=None):
        receiving = action == "wait_recv"
        for kind in kinds:
            ok = neighbours[opposite[kind] if receiving else kind][0]
            if step:
                ok = ok & (has_earlier if receiving else has_later)
            crossing = is_far(kind, receiving)
            if far_ones is not None:
                if crossing is None:
                    continue
                ok = ok & (crossing if far_ones else ~crossing)

            @pl.when(ok)
            def _(kind=kind):
                source = border.at[l // 3, pl.ds(0, BX)] if far_ones and l % 3 == 2 else None
                getattr(edge(l, kind, step, source), action)()

    def shift(l, kind):
        if kind == STRIP:
            rows, body = pl.ds(jnp.where(far_up, R1 - 8, R0), 8), pl.ds(X0, BX)
        else:
            rows = pl.ds(jnp.where(far_up, R0, R0 + 8), ROWS - 8)
            body = {LOW: pl.ds(X0, 4), HIGH: pl.ds(X0 + BX - 4, 4), REST: pl.ds(X0 + 4, BX - 8)}[kind]
        return remote(u.at[l, body, rows], u.at[l + 1, body, rows], l, kind, later)

    def each_shift(action, l, kind):
        @pl.when(has_earlier if action == "wait_recv" else has_later)
        def _():
            getattr(shift(l, kind), action)()

    def tendency(l, write, r0=R0, rows=ROWS, begin=X0, end=X0 + BX, unroll=4):
        last_lane, first_lane, bottom, top, forward_x, forward_y, wind_x, wind_y, wind_both = constants(rows)

        def weights(x, carry):
            v = u[l, x, pl.ds(r0 - 2, rows + 4), :]
            h[x, pl.ds(r0 - 2, rows + 4), :] = 0.75 - 0.5 / (1.0 + v * v)
            return carry

        def row(x, carry):
            def at(dx, dr):
                return u[l, x + dx, pl.ds(r0 + dr, rows), :]

            def weight(dx, dr):
                return h[x + dx, pl.ds(r0 + dr, rows), :]

            c, hc = at(0, 0), weight(0, 0)
            xm, xp, ym, yp = at(-1, 0), at(1, 0), at(0, -2), at(0, 2)
            spread = (hc + weight(1, 0)) * (xp - c) + (hc + weight(-1, 0)) * (xm - c)
            spread = spread + ((hc + weight(0, 2)) * (yp - c) + (hc + weight(0, -2)) * (ym - c))
            near_x = jnp.where(forward_x, xm, xp)
            far_x = jnp.where(forward_x, at(-2, 0), at(2, 0))
            near_y = jnp.where(forward_y, ym, yp)
            far_y = jnp.where(forward_y, at(0, -4), at(0, 4))
            carried = wind_x * (far_x - 4.0 * near_x) + wind_y * (far_y - 4.0 * near_y) + wind_both * c
            below = jnp.where(bottom, c, pltpu.roll(jnp.where(last_lane, at(0, -1), c), 1, axis=1))
            above = jnp.where(top, c, pltpu.roll(jnp.where(first_lane, at(0, 1), c), 127, axis=1))
            rate = strength * spread - carried + vm[x - X0, pl.ds(r0 - R0, rows), :] * (below + above - 2.0 * c)
            write(x, c, rate)
            return carry

        if begin is None:
            for x in (1, 2, 3, 4, BX - 1, BX, BX + 1, BX + 2):
                weights(x, 0)
            for x in (X0, X0 + 1, BX, BX + 1):
                row(x, 0)
        else:
            lax.fori_loop(begin - 1, end + 1, weights, 0, unroll=2)
            lax.fori_loop(begin, end, row, 0, unroll=unroll)

    def initial(x, c, rate):
        c1[x - X0] = A[0] * rate + A[1] * rate + A[2] * rate
        c2[x - X0] = B[0] * rate + B[1] * rate + B[2] * rate

    def to_middle(l, out):
        def write(x, c, rate):
            state = c + half_step * rate + c1[x - X0]
            u[l, x, pl.ds(R0, ROWS), :] = state
            if out is None:
                p1[x - X0] = rate
            else:
                out[x - X0] = state
        return write

    def to_final(l, r0, rows):
        own = pl.ds(r0 - R0, rows)

        def write(x, c, rate):
            u[l, x, pl.ds(r0, rows), :] = c + half_step * rate + c2[x - X0, own, :]
            g0 = p1[x - X0, own, :]
            p1[x - X0, own, :] = A[0] * g0 + A[1] * rate
            p2[x - X0, own, :] = B[0] * g0 + B[1] * rate
        return write

    def finish(x, c, rate):
        c1[x - X0] = p1[x - X0] + A[2] * rate
        c2[x - X0] = p2[x - X0] + B[2] * rate

    def last(r0, rows):
        own = pl.ds(r0 - R0, rows)

        def write(x, c, rate):
            final_out[x - X0, own, :] = c + half_step * rate + c2[x - X0, own, :]
        return write

    def copy_start():
        def body(x, carry):
            rows = pl.ds(R0 - 8, ROWS + 16)
            for l in (1, 4, 7):
                u[l, x, rows, :] = u[0, x, rows, :]
            return carry

        @pl.when(~has_earlier)
        def _():
            lax.fori_loop(0, BX + 4, body, 0, unroll=2)

    def border_first(sweep, end):
        def run(r0, kind):
            rows = pl.ds(r0 - R0, 4)

            def slopes(x, c, rate):
                if sweep == 0:
                    border_c[x - X0] = A[0] * rate + A[1] * rate + A[2] * rate
                else:
                    border_c[x - X0] = p1[x - X0, rows, :] + A[2] * rate

            def state(x, c, rate):
                border[sweep, x - X0] = c + half_step * rate + border_c[x - X0]

            each_edge("wait_recv", end, (opposite[kind],))
            tendency(end, slopes, r0, 4, unroll=8)
            if sweep == 0:
                copy_start()
            each_shift("wait_recv", end, STRIP)
            each_edge("wait_recv", end, (XUP, XDOWN, opposite[kind]), step=1)
            tendency(end + 1, state, r0, 4, unroll=8)

        each_edge("wait_recv", end, (YUP, YDOWN), far_ones=False)

        @pl.when(far_up)
        def _():
            run(R1 - 4, YUP)

        @pl.when(far_down)
        def _():
            run(R0, YDOWN)

        if sweep == 0:
            @pl.when(~far)
            def _():
                copy_start()

    for sweep in range(3):
        end, first, middle = 3 * sweep, 3 * sweep + 1, 3 * sweep + 2
        each_edge("start", end, (YUP, YDOWN), far_ones=True)
        each_edge("start", end, (YUP, YDOWN), step=1, far_ones=True)
        each_edge("start", end, (XUP, XDOWN), step=1)
        each_edge("start", end, (XUP, XDOWN))
        each_edge("start", end, (YUP, YDOWN), far_ones=False)
        each_shift("start", end, STRIP)
        each_edge("start", end, (YUP, YDOWN), step=1, far_ones=False)
        each_edge("wait_recv", end, (XUP, XDOWN))
        for kind in (LOW, HIGH, REST):
            each_shift("start", end, kind)
        border_first(sweep, end)
        each_edge("start", middle, (YUP, YDOWN), far_ones=True)
        tendency(end, initial if sweep == 0 else finish)

        @pl.when(~far)
        def _():
            each_shift("wait_recv", end, STRIP)
            each_edge("wait_recv", end, (XUP, XDOWN), step=1)

        each_edge("wait_recv", end, (YUP, YDOWN), step=1, far_ones=False)
        each_shift("wait_recv", end, LOW)
        each_shift("wait_recv", end, HIGH)
        write = to_middle(middle, middle_out if sweep == 2 else None)
        tendency(first, write, begin=None)
        each_edge("start", middle, (XUP, XDOWN))
        each_shift("wait_recv", end, REST)
        tendency(first, write, begin=X0 + 2, end=X0 + BX - 2)
        each_edge("start", middle, (YUP, YDOWN), far_ones=False)
        each_edge("wait_recv", middle, (XUP, XDOWN))
        each_edge("wait_recv", middle, (YUP, YDOWN), far_ones=False)

        def part(r0, rows, unroll=4):
            write = to_final(middle + 1, r0, rows) if sweep < 2 else last(r0, rows)
            tendency(middle, write, r0, rows, unroll=unroll)

        @pl.when(~far)
        def _():
            part(R0, ROWS)

        @pl.when(far_up)
        def _():
            part(R0, ROWS - 4)
            each_edge("wait_recv", middle, (YDOWN,))
            part(R1 - 4, 4, 8)

        @pl.when(far_down)
        def _():
            part(R0 + 4, ROWS - 4)
            each_edge("wait_recv", middle, (YUP,))
            part(R0, 4, 8)

    for end in (0, 3, 6):
        each_edge("wait_send", end)
        each_edge("wait_send", end, step=1)
        for kind in (STRIP, LOW, HIGH, REST):
            each_shift("wait_send", end, kind)
        each_edge("wait_send", end + 2, (XUP, XDOWN))
        each_edge("wait_send", end + 2, (YUP, YDOWN), far_ones=False)
        each_edge("wait_send", end + 2, (YUP, YDOWN), far_ones=True)


def unpack(middle, final, middle_out, final_out):
    def body(x, carry):
        for source, target in ((middle, middle_out), (final, final_out)):
            for half in range(2):
                target[0, x, :, pl.ds(128 * half, 128)] = source[x, pl.ds(half, BY, stride=2), :]
        return carry

    lax.fori_loop(0, BX, body, 0, unroll=4)


def solution(mesh):
    shape = tuple(mesh.shape[a] for a in ("tm", "gx", "gy"))

    def shards(start_states, wind_code, wind_profile, vertical_mix):
        block = jax.ShapeDtypeStruct(start_states.shape, jnp.float32)
        packed = jax.ShapeDtypeStruct((BX + 1, ROWS, 128), jnp.float32)
        field = pltpu.VMEM(packed.shape, jnp.float32)
        any_space, vmem = pl.BlockSpec(memory_space=pl.ANY), pl.BlockSpec(memory_space=pltpu.VMEM)
        middle, final = pl.pallas_call(
            lambda *refs: kernel(shape, *refs),
            out_shape=(packed, packed),
            in_specs=[any_space, pl.BlockSpec(memory_space=pltpu.SMEM), any_space, any_space],
            out_specs=(vmem, vmem),
            scratch_shapes=[
                pltpu.VMEM((FIELDS, BX + 4, ROWS + 32, 128), jnp.float32),
                pltpu.VMEM((BX + 4, ROWS + 32, 128), jnp.float32),
                field, field, field, field, field,
                pltpu.VMEM((3, BX + 1, 4, 128), jnp.float32),
                pltpu.VMEM((BX + 1, 4, 128), jnp.float32),
                pltpu.VMEM((2, 2, BX, BY, 128), jnp.float32),
                pltpu.VMEM((2, 256), jnp.float32),
                pltpu.SemaphoreType.DMA,
                pltpu.SemaphoreType.DMA((2, 2)),
                pltpu.SemaphoreType.DMA((FIELDS, NEXT + 4)),
                pltpu.SemaphoreType.DMA((FIELDS, NEXT + 4)),
            ],
            compiler_params=pltpu.CompilerParams(collective_id=0, has_side_effects=True, vmem_limit_bytes=54000 * 1024),
        )(start_states, wind_code, pltpu.with_memory_space_constraint(wind_profile, pltpu.HBM), vertical_mix)
        return pl.pallas_call(
            unpack,
            out_shape=(block, block),
            in_specs=[vmem, vmem],
            out_specs=(vmem, vmem),
            compiler_params=pltpu.CompilerParams(vmem_limit_bytes=8 * 1024 * 1024),
        )(middle, final)

    in_specs = (P("tm", "gx", "gy", None), P("gx", "gy"), P(), P("gx", "gy", None))
    out_specs = (P("tm", "gx", "gy", None), P("tm", "gx", "gy", None))
    return jax.shard_map(shards, mesh=mesh, in_specs=in_specs, out_specs=out_specs, check_vma=False)
```
